32 devices in a mesh: ctx: 8 (over y, x, core), head: 4 (over z).
Axes of the slice: x: 2, y: 2, z: 4, core: 2. Of those that a mesh axis runs over, the one named last changes fastest.
Arguments:
- queries: bfloat16 [2048, 4096], P('ctx', 'head'), may hold values from -6 to 6
- key_rows: bfloat16 [2048, 4096], P('ctx', 'head'), may hold values from -6 to 6
- value_rows: bfloat16 [2048, 4096], P('ctx', 'head'), may hold values from -6 to 6
- out_weight: bfloat16 [4096, 4096], P('head'), may hold values from -0.125 to 0.125
- cotangent: bfloat16 [2048, 4096], P('ctx', 'head'), may hold values from -6 to 6
Outputs:
- mixed: bfloat16 [2048, 4096], P('ctx', 'head')
- grad_queries: bfloat16 [2048, 4096], P('ctx', 'head')
- grad_keys: bfloat16 [2048, 4096], P('ctx', 'head')
- grad_values: bfloat16 [2048, 4096], P('ctx', 'head')
- grad_out_weight: float32 [4096, 4096], P('head', 'ctx')
The draws below stay inside these ranges and needn't reach their ends.
All inputs are finite; a program needn't handle non-finite values.
Results may differ from the reference program's by a relative error of at most 0.0052.
Values may be sent and summed in bfloat16 or wider, within the bound.
No kernel may reach another device: no remote copies, remote signals or barrier semaphores. Data moves between devices by JAX's collectives and lax.ppermute only.
A program may use at most 64 MiB of HBM per device.

```python
import jax
import jax.numpy as jnp
from jax import lax

D = 4096
HEADS = 32
HEAD_DIM = 128
TOK_DEV = 256
TOKENS = 2048
N_CTX = 8


def with_spikes(drawn, stream_key, source, target, blocks, factor):
    def block_of(position):
        return (jnp.arange(drawn.shape[position]) // (drawn.shape[position] // blocks)).reshape((-1,) + (1,) * (drawn.ndim - 1 - position))

    one_side = jax.random.permutation(stream_key, blocks)[block_of(target)]
    other_side = (block_of(target) + blocks // 2) % blocks
    return jnp.where((block_of(source) == one_side) | (block_of(source) == other_side), factor * drawn, drawn)


def levels(rng, shape, cuts, low, high):
    def one(axis_at, shards_of):
        steps = jax.random.uniform(jax.random.fold_in(jax.random.fold_in(rng, 6), axis_at), (shards_of,), jnp.float32, low / len(cuts), high / len(cuts))
        return jnp.repeat(jnp.exp(steps), shape[axis_at] // shards_of).reshape((-1,) + (1,) * (len(shape) - axis_at - 1))

    factor_of = one(*cuts[0])
    for cut in cuts[1:]:
        factor_of = factor_of * one(*cut)
    return factor_of


def centred(key, dims, deviation, reach, cuts=(), dtype=jnp.bfloat16):
    factor_of = levels(key, dims, cuts, -0.22, 0.18) if cuts else 1.0
    array = jax.random.normal(key, dims, jnp.float32) * deviation * factor_of
    return jnp.minimum(jnp.maximum(array, -reach), reach).astype(dtype)


def noise_with(own_key, extent, spread, most, shards, heavy, held_as=jnp.bfloat16):
    drawn = spread * jax.random.normal(own_key, extent, jnp.float32)
    if shards:
        drawn = drawn * levels(own_key, extent, shards, -0.22, 0.18)
    return jnp.clip(with_spikes(drawn, jax.random.fold_in(own_key, 3), *heavy), -most, most).astype(held_as)


def setup_inputs(seed: int = 0) -> dict:
    seeds = jax.random.split(jax.random.key(seed), 6)
    return {
        "queries": centred(seeds[0], (TOKENS, HEADS * HEAD_DIM), 1.0, 6.0, ((0, 8), (1, 4))),
        "key_rows": centred(seeds[1], (TOKENS, HEADS * HEAD_DIM), 1.0, 6.0, ((0, 8), (1, 4))),
        "value_rows": centred(seeds[2], (TOKENS, HEADS * HEAD_DIM), 1.0, 6.0, ((0, 8), (1, 4))),
        "out_weight": noise_with(seeds[3], (HEADS * HEAD_DIM, D), (HEADS * HEAD_DIM) ** -0.5, 0.125, ((0, 4),), (0, 1, 4, 2.0)),
        "cotangent": centred(seeds[4], (TOKENS, D), 1.0, 6.0, ((0, 8), (1, 4))),
    }


epsilon = 1e-06

def split_heads(matrix):
    return matrix.reshape(N_CTX, TOK_DEV, HEADS, HEAD_DIM)

def reference(queries, key_rows, value_rows, out_weight, cotangent):
    query_blocks = split_heads(queries)
    key_blocks = split_heads(key_rows)
    value_blocks = split_heads(value_rows)
    causal = jnp.arange(TOK_DEV)[:, None] >= jnp.arange(TOK_DEV)[None, :]
    highest = lax.Precision.HIGHEST

    def block_scores(query_wide, key_wide):
        scores = jnp.einsum('thd,shd->hts', query_wide, key_wide)
        return jnp.where(causal[None], scores, 0.0).astype(jnp.bfloat16)

    def forward_step(running, blocks):
        query_now, key_now, value_now = blocks
        query_wide = query_now.astype(jnp.float32)
        key_wide = key_now.astype(jnp.float32)
        value_wide = value_now.astype(jnp.float32)
        scores = block_scores(query_wide, key_wide)
        attended = jnp.einsum('hts,she->the', scores.astype(jnp.float32), value_wide)
        attended = attended + jnp.einsum('thd,hde->the', query_wide, running, precision=highest)
        block_state = jnp.einsum('thd,the->hde', key_wide, value_wide)
        return (running + block_state, (attended, running))
    zero_state = jnp.zeros((HEADS, HEAD_DIM, HEAD_DIM), jnp.float32)
    _, (attended, prefix_states) = lax.scan(forward_step, zero_state, (query_blocks, key_blocks, value_blocks))
    row_scale = lax.rsqrt(lax.optimization_barrier(jnp.mean(attended * attended, axis=-1, keepdims=True)) + epsilon)
    unit_rows = attended * row_scale
    normed = unit_rows.astype(jnp.bfloat16).reshape(TOKENS, HEADS * HEAD_DIM)
    mixed = jnp.dot(normed, out_weight, preferred_element_type=jnp.float32).astype(jnp.bfloat16)
    upstream = jnp.dot(cotangent, out_weight.T, preferred_element_type=jnp.float32)
    upstream = upstream.reshape(N_CTX, TOK_DEV, HEADS, HEAD_DIM)
    d_attended = row_scale * (upstream - unit_rows * lax.optimization_barrier(jnp.mean(upstream * unit_rows, axis=-1, keepdims=True)))
    d_attended = d_attended.astype(jnp.bfloat16)

    def backward_step(running, blocks):
        query_now, key_now, value_now, grad_now, prefix_now = blocks
        query_wide = query_now.astype(jnp.float32)
        key_wide = key_now.astype(jnp.float32)
        value_wide = value_now.astype(jnp.float32)
        grad_wide = grad_now.astype(jnp.float32)
        scores = block_scores(query_wide, key_wide).astype(jnp.float32)
        back_scores = jnp.einsum('the,she->hts', grad_wide, value_wide)
        back_scores = jnp.where(causal[None], back_scores, 0.0).astype(jnp.bfloat16).astype(jnp.float32)
        grad_q = jnp.einsum('hts,shd->thd', back_scores, key_wide)
        grad_q = grad_q + jnp.einsum('the,hde->thd', grad_wide, prefix_now, precision=highest)
        grad_k = jnp.einsum('hts,thd->shd', back_scores, query_wide)
        grad_k = grad_k + jnp.einsum('she,hde->shd', value_wide, running, precision=highest)
        grad_v = jnp.einsum('hts,the->she', scores, grad_wide)
        grad_v = grad_v + jnp.einsum('shd,hde->she', key_wide, running, precision=highest)
        grad_block = jnp.einsum('thd,the->hde', query_wide, grad_wide)
        outputs = (grad_q.astype(jnp.bfloat16), grad_k.astype(jnp.bfloat16), grad_v.astype(jnp.bfloat16))
        return (running + grad_block, outputs)
    _, (grad_q, grad_k, grad_v) = lax.scan(backward_step, zero_state, (query_blocks, key_blocks, value_blocks, d_attended, prefix_states), reverse=True)
    grad_out_weight = jnp.dot(normed.T, cotangent, preferred_element_type=jnp.float32)
    width = HEADS * HEAD_DIM
    return (mixed, grad_q.reshape(TOKENS, width), grad_k.reshape(TOKENS, width), grad_v.reshape(TOKENS, width), grad_out_weight)
```

```python
import jax
import jax.numpy as jnp
from jax import lax
from jax.sharding import PartitionSpec as P

HEAD_DIM = 128

epsilon = 1e-06


bf16 = jnp.bfloat16
f32 = jnp.float32


def dot_f32(spec, a, b):
    return jnp.einsum(spec, a, b, preferred_element_type=f32)


def split_dot(spec, a, b):
    high = b.astype(bf16)
    low = (b - high.astype(f32)).astype(bf16)
    return dot_f32(spec, a, high) + dot_f32(spec, a, low)


def flipped(size, mask):
    return [(i, i ^ mask) for i in range(size)]


def bits_of(size):
    mask = 1
    while mask < size:
        yield mask
        mask *= 2


def exclusive_sum(block, position, size, upward):
    total = block
    outer = jnp.zeros_like(block)
    for mask in bits_of(size):
        other = lax.ppermute(total.astype(bf16), "ctx", flipped(size, mask)).astype(f32)
        upper = (position & mask) != 0
        take = upper if upward else jnp.logical_not(upper)
        outer = outer + jnp.where(take, other, 0.0)
        total = total + other
    return outer


def gather_line(block, place, size):
    right = left = block
    rights, lefts = [None] * size, [None] * size
    for r in range(1, size):
        right = lax.ppermute(right, "head", [(i, i + 1) for i in range(r - 1, size - 1)])
        left = lax.ppermute(left, "head", [(i, i - 1) for i in range(1, size - r + 1)])
        rights[r], lefts[r] = right, left
    slots = [block]
    for r in range(1, size):
        slots.append(jnp.where(place >= r, rights[r], lefts[size - r]))
    return slots


def scatter_line(piece, size):
    right = left = None
    for r in range(1, size):
        send_right = piece(size - r) if right is None else piece(size - r) + right
        send_left = piece(r) if left is None else piece(r) + left
        right = lax.ppermute(
            send_right.astype(bf16), "head", [(i, i + 1) for i in range(min(r, size - 1))]
        ).astype(f32)
        left = lax.ppermute(
            send_left.astype(bf16), "head", [(i, i - 1) for i in range(max(1, size - r), size)]
        ).astype(f32)
    own = piece(0)
    return own if right is None else own + right + left


def make_body(n_ctx, n_head):
    def body(queries, key_rows, value_rows, out_weight, cotangent):
        length, width = queries.shape
        heads_here = width // HEAD_DIM
        model = out_weight.shape[1]
        part = model // n_head
        position = lax.axis_index("ctx")
        place = lax.axis_index("head")
        q = queries.reshape(length, heads_here, HEAD_DIM)
        k = key_rows.reshape(length, heads_here, HEAD_DIM)
        v = value_rows.reshape(length, heads_here, HEAD_DIM)
        causal = lax.broadcasted_iota(jnp.int32, (length, length), 0) >= lax.broadcasted_iota(
            jnp.int32, (length, length), 1
        )

        def weight_part(s):
            start = lax.rem(place + s, n_head) * part
            return lax.dynamic_slice(out_weight, (0, start), (width, part))

        slots = gather_line(cotangent, place, n_head)

        block_state = dot_f32("thd,the->hde", k, v)
        scores = dot_f32("thd,shd->hts", q, k)
        scores = jnp.where(causal[None], scores, 0.0).astype(bf16)
        attended = dot_f32("hts,she->the", scores, v)
        prefix_state = exclusive_sum(block_state, position, n_ctx, True)
        attended = attended + split_dot("thd,hde->the", q, prefix_state)
        row_scale = lax.rsqrt(jnp.mean(attended * attended, axis=-1, keepdims=True) + epsilon)
        unit_rows = attended * row_scale
        normed = unit_rows.astype(bf16).reshape(length, width)

        mixed = scatter_line(lambda s: jnp.dot(normed, weight_part(s), preferred_element_type=f32), n_head)
        mixed = mixed.astype(bf16)

        upstream = None
        for r, slot in enumerate(slots):
            term = lax.dot_general(
                slot, weight_part(n_head - r), (((1,), (1,)), ((), ())), preferred_element_type=f32
            )
            upstream = term if upstream is None else upstream + term
        upstream = upstream.reshape(length, heads_here, HEAD_DIM)
        d_attended = row_scale * (
            upstream - unit_rows * jnp.mean(upstream * unit_rows, axis=-1, keepdims=True)
        )
        d_attended = d_attended.astype(bf16)
        grad_block = dot_f32("thd,the->hde", q, d_attended)
        suffix_state = exclusive_sum(grad_block, position, n_ctx, False)
        back_scores = dot_f32("the,she->hts", d_attended, v)
        back_scores = jnp.where(causal[None], back_scores, 0.0).astype(bf16)
        grad_q = dot_f32("hts,shd->thd", back_scores, k)
        grad_q = grad_q + split_dot("the,hde->thd", d_attended, prefix_state)
        grad_k = dot_f32("hts,thd->shd", back_scores, q)
        grad_k = grad_k + split_dot("she,hde->shd", v, suffix_state)
        grad_v = dot_f32("hts,the->she", scores, d_attended)
        grad_v = grad_v + split_dot("shd,hde->she", k, suffix_state)

        pair = min(2, n_ctx)
        chips = n_ctx // pair
        chip_cols = model // chips
        stacked = jnp.stack(slots)

        def columns_of(chip):
            if chip_cols <= part:
                start = chip * chip_cols
                slot = lax.rem(place - start // part + n_head, n_head)
                got = lax.dynamic_slice(stacked, (slot, 0, lax.rem(start, part)), (1, length, chip_cols))
                return got[0]
            each = chip_cols // part
            taken = []
            for n in range(each):
                slot = lax.rem(place - (chip * each + n) + n_head, n_head)
                taken.append(lax.dynamic_index_in_dim(stacked, slot, 0, keepdims=False))
            return jnp.concatenate(taken, axis=1)

        rows, cols = [normed], [columns_of(position // pair)]
        for m in range(pair, n_ctx, pair):
            perm = flipped(n_ctx, m)
            rows.append(lax.ppermute(normed, "ctx", perm))
            cols.append(lax.ppermute(columns_of((position ^ m) // pair), "ctx", perm))
        rows = jnp.concatenate(rows, axis=0)
        cols = jnp.concatenate(cols, axis=0)
        own_cols = chip_cols // pair

        def grad_part(core):
            taken = lax.dynamic_slice(cols, (0, core * own_cols), (cols.shape[0], own_cols))
            return lax.dot_general(rows, taken, (((0,), (0,)), ((), ())), preferred_element_type=f32)

        core = lax.rem(position, pair)
        grad_out_weight = grad_part(core)
        if pair > 1:
            other = lax.ppermute(grad_part(1 - core).astype(bf16), "ctx", flipped(n_ctx, 1))
            grad_out_weight = grad_out_weight + other.astype(f32)
        return (
            mixed,
            grad_q.astype(bf16).reshape(length, width),
            grad_k.astype(bf16).reshape(length, width),
            grad_v.astype(bf16).reshape(length, width),
            grad_out_weight,
        )

    return body


def solution(mesh):
    return jax.shard_map(
        make_body(mesh.shape["ctx"], mesh.shape["head"]),
        mesh=mesh,
        in_specs=(P("ctx", "head"),) * 3 + (P("head", None), P("ctx", "head")),
        out_specs=(P("ctx", "head"),) * 4 + (P("head", "ctx"),),
        check_vma=False,
    )
```

```python
import functools

import jax
import jax.numpy as jnp
from jax import lax
from jax.experimental import pallas as pl
from jax.experimental.pallas import tpu as pltpu
from jax.sharding import PartitionSpec as P


HEAD_DIM = 128

epsilon = 1e-06


bf16 = jnp.bfloat16
f32 = jnp.float32
VMEM = pl.BlockSpec(memory_space=pltpu.VMEM)
GRANT = 24 << 20


def mm(a, b, da, db):
    return lax.dot_general(a, b, (((da,), (db,)), ((), ())), preferred_element_type=f32)


def split(x):
    high = x.astype(bf16)
    return high, (x - high.astype(f32)).astype(bf16)


def head(h):
    return slice(h * HEAD_DIM, (h + 1) * HEAD_DIM)


def below(n):
    return lax.broadcasted_iota(jnp.int32, (n, n), 0) >= lax.broadcasted_iota(jnp.int32, (n, n), 1)


def array(shape, dtype):
    return jax.ShapeDtypeStruct(shape, dtype)


def kernel_call(kernel, *args, **settings):
    return pl.pallas_call(kernel, compiler_params=pltpu.CompilerParams(vmem_limit_bytes=GRANT), **settings)(*args)


def call(kernel, outs, *args):
    return kernel_call(
        kernel, *args, out_shape=outs, in_specs=[VMEM] * len(args), out_specs=jax.tree.map(lambda _: VMEM, outs)
    )


def state_kernel(k, v, out):
    for h in range(k.shape[1] // HEAD_DIM):
        out[head(h), :] = mm(k[:, head(h)], v[:, head(h)], 0, 0)


def intra_kernel(q, k, v, out):
    keep = below(q.shape[0])
    for h in range(q.shape[1] // HEAD_DIM):
        scores = jnp.where(keep, mm(q[:, head(h)], k[:, head(h)], 1, 1), 0.0).astype(bf16)
        out[:, head(h)] = mm(scores, v[:, head(h)], 1, 0)


def row_scale_of(attended):
    return lax.rsqrt(jnp.mean(attended * attended, axis=-1, keepdims=True) + epsilon)


def norm_kernel(q, intra, prefix, attended, normed):
    for h in range(q.shape[1] // HEAD_DIM):
        high, low = split(prefix[head(h), :])
        query = q[:, head(h)]
        value = intra[:, head(h)] + mm(query, high, 1, 0) + mm(query, low, 1, 0)
        attended[:, head(h)] = value
        normed[:, head(h)] = (value * row_scale_of(value)).astype(bf16)


def pieces_kernel(count, rounded, _, normed, *refs):
    weights, outs = refs[:count], refs[count:]
    for n in range(count):
        value = mm(normed[...], weights[n][...], 1, 0)
        outs[n][...] = value
        if rounded:
            outs[count + n][...] = value.astype(bf16)


def upstream_kernel(count, _, *refs):
    slots, weights, out = refs[:count], refs[count : 2 * count], refs[2 * count]
    value = mm(slots[0][...], weights[0][...], 1, 1)
    for n in range(1, count):
        value = value + mm(slots[n][...], weights[n][...], 1, 1)
    out[...] = value


def finish_kernel(count, _, *refs):
    slots, weights = refs[:count], refs[count : 2 * count]
    so_far, attended, q, d_out, grad_out = refs[2 * count :]
    upstream = so_far[...]
    for n in range(count):
        upstream = upstream + mm(slots[n][...], weights[n][...], 1, 1)
    for h in range(d_out.shape[1] // HEAD_DIM):
        value, up = attended[:, head(h)], upstream[:, head(h)]
        scale = row_scale_of(value)
        unit = value * scale
        grad = scale * (up - unit * jnp.mean(up * unit, axis=-1, keepdims=True))
        grad = grad.astype(bf16)
        d_out[:, head(h)] = grad
        grad_out[head(h), :] = mm(q[:, head(h)], grad, 0, 0)


def back_kernel(q, k, v, d, prefix, grad_q, part_k, part_v):
    keep = below(q.shape[0])
    for h in range(q.shape[1] // HEAD_DIM):
        qh, kh, vh, dh = q[:, head(h)], k[:, head(h)], v[:, head(h)], d[:, head(h)]
        high, low = split(prefix[head(h), :])
        scores = jnp.where(keep, mm(qh, kh, 1, 1), 0.0).astype(bf16)
        back = jnp.where(keep, mm(dh, vh, 1, 1), 0.0).astype(bf16)
        grad_q[:, head(h)] = (mm(back, kh, 1, 0) + mm(dh, high, 1, 1) + mm(dh, low, 1, 1)).astype(bf16)
        part_k[:, head(h)] = mm(back, qh, 0, 0)
        part_v[:, head(h)] = mm(scores, dh, 0, 0)


def suffix_kernel(k, v, part_k, part_v, suffix, grad_k, grad_v):
    for h in range(k.shape[1] // HEAD_DIM):
        high, low = split(suffix[head(h), :])
        kh, vh = k[:, head(h)], v[:, head(h)]
        grad_k[:, head(h)] = (part_k[:, head(h)] + mm(vh, high, 1, 1) + mm(vh, low, 1, 1)).astype(bf16)
        grad_v[:, head(h)] = (part_v[:, head(h)] + mm(kh, high, 1, 0) + mm(kh, low, 1, 0)).astype(bf16)


def weight_grad_kernel(count, adds, _, *refs):
    rows, cols = refs[:count], refs[count : 2 * count]
    out = refs[-1]
    value = mm(rows[0][...], cols[0][...], 0, 0)
    for n in range(1, count):
        value = value + mm(rows[n][...], cols[n][...], 0, 0)
    if adds:
        value = value + refs[2 * count][...].astype(f32)
    out[...] = value.astype(out.dtype)


def flipped(size, mask):
    return [(i, i ^ mask) for i in range(size)]


def shifted(size, by):
    return [(i, (i + by) % size) for i in range(size)]


def exclusive_sum(block, position, size, upward):
    total = block
    outer = jnp.zeros_like(block)
    mask = 1
    while mask < size:
        sent = total if mask == 1 else total.astype(bf16)
        other = lax.ppermute(sent, "ctx", flipped(size, mask))
        other = other.astype(f32)
        upper = (position & mask) != 0
        take = upper if upward else jnp.logical_not(upper)
        outer = outer + jnp.where(take, other, 0.0)
        total = total + other
        mask *= 2
    return outer


def make_body(n_ctx, n_head):
    pair = min(2, n_ctx)
    chips = n_ctx // pair

    def body(queries, key_rows, value_rows, out_weight, cotangent):
        length, width = queries.shape
        heads_here = width // HEAD_DIM
        model = out_weight.shape[1]
        part = model // n_head
        chip_cols = model // chips
        own_cols = chip_cols // pair
        tiles = 2 if heads_here % 2 == 0 else 1
        position = lax.axis_index("ctx")
        place = lax.axis_index("head")
        place_at = place.reshape(1).astype(jnp.int32)

        slots = [cotangent]
        for r in range(1, n_head):
            slots.append(lax.ppermute(cotangent, "head", shifted(n_head, r)))

        block_state = call(state_kernel, array((width, HEAD_DIM), f32), key_rows, value_rows)
        intra = call(intra_kernel, array((length, width), f32), queries, key_rows, value_rows)
        prefix = exclusive_sum(block_state, position, n_ctx, True)
        attended, normed = call(
            norm_kernel, (array((length, width), f32), array((length, width), bf16)), queries, intra, prefix
        )

        def pieces(steps, rounded):
            steps = tuple(steps)
            tile = part // tiles
            blocks = [
                pl.BlockSpec(
                    (width, tile),
                    functools.partial(lambda s, i, at: (0, lax.rem(at[0] + s, n_head) * tiles + i), s),
                )
                for s in steps
            ]
            out = pl.BlockSpec((length, tile), lambda i, at: (0, i))
            copies = 2 if rounded else 1
            got = kernel_call(
                functools.partial(pieces_kernel, len(steps), rounded),
                place_at,
                normed,
                *([out_weight] * len(steps)),
                out_shape=[array((length, part), f32)] * len(steps)
                + [array((length, part), bf16)] * (len(steps) if rounded else 0),
                grid_spec=pltpu.PrefetchScalarGridSpec(
                    num_scalar_prefetch=1,
                    grid=(tiles,),
                    in_specs=[pl.BlockSpec((length, width), lambda i, at: (0, 0))] + blocks,
                    out_specs=[out] * (len(steps) * copies),
                ),
            )
            wide = dict(zip(steps, got[: len(steps)]))
            return wide, dict(zip(steps, got[len(steps) :]))

        first = sorted({1, n_head - 1} - {0}) if n_head > 1 else []
        wide, narrow = pieces(first, True) if first else ({}, {})
        rest = [s for s in range(n_head) if s not in first]
        wide_rest, _ = pieces(rest, False)
        wide = {**wide, **wide_rest}
        right = left = None
        for r in range(1, n_head):
            if r == 1:
                send_right, send_left = narrow[n_head - 1], narrow[1]
            else:
                send_right = (wide[n_head - r] + right).astype(bf16)
                send_left = (wide[r] + left).astype(bf16)
            right = lax.ppermute(
                send_right, "head", [(i, i + 1) for i in range(min(r, n_head - 1))]
            ).astype(f32)
            left = lax.ppermute(send_left, "head", [(i, i - 1) for i in range(max(1, n_head - r), n_head)]).astype(f32)
        mixed = wide[0] if right is None else wide[0] + right + left
        mixed = mixed.astype(bf16)

        perms = [flipped(n_ctx, m) for m in range(pair, n_ctx, pair)]
        rows = [normed]
        for perm in perms:
            rows.append(lax.ppermute(normed, "ctx", perm))

        def weight_specs(which):
            return [
                pl.BlockSpec(
                    (width // tiles, part),
                    functools.partial(lambda r, i, at: (i, lax.rem(at[0] + n_head - r, n_head)), r),
                )
                for r in which
            ]

        late = [n_head // 2] if n_head > 1 else []
        early = [r for r in range(n_head) if r not in late]
        slot_spec = pl.BlockSpec((length, part), lambda i, at: (0, 0))
        tile_spec = pl.BlockSpec((length, width // tiles), lambda i, at: (0, i))
        so_far = kernel_call(
            functools.partial(upstream_kernel, len(early)),
            place_at,
            *[slots[r] for r in early],
            *([out_weight] * len(early)),
            out_shape=array((length, width), f32),
            grid_spec=pltpu.PrefetchScalarGridSpec(
                num_scalar_prefetch=1,
                grid=(tiles,),
                in_specs=[slot_spec] * len(early) + weight_specs(early),
                out_specs=tile_spec,
            ),
        )
        d_attended, grad_block = kernel_call(
            functools.partial(finish_kernel, len(late)),
            place_at,
            *[slots[r] for r in late],
            *([out_weight] * len(late)),
            so_far,
            attended,
            queries,
            out_shape=(array((length, width), bf16), array((width, HEAD_DIM), f32)),
            grid_spec=pltpu.PrefetchScalarGridSpec(
                num_scalar_prefetch=1,
                grid=(tiles,),
                in_specs=[slot_spec] * len(late) + weight_specs(late) + [tile_spec] * 3,
                out_specs=(tile_spec, pl.BlockSpec((width // tiles, HEAD_DIM), lambda i, at: (i, 0))),
            ),
        )

        def columns_of(chip):
            if chip_cols == part:
                slot = lax.rem(place - chip + n_head, n_head)
                got = slots[0]
                for r in range(1, n_head):
                    got = jnp.where(slot == r, slots[r], got)
                return got
            stacked = jnp.stack(slots)
            if chip_cols < part:
                start = chip * chip_cols
                slot = lax.rem(place - start // part + n_head, n_head)
                at = (slot, 0, lax.rem(start, part))
                return lax.dynamic_slice(stacked, at, (1, length, chip_cols))[0]
            each = chip_cols // part
            taken = []
            for n in range(each):
                slot = lax.rem(place - (chip * each + n) + n_head, n_head)
                taken.append(lax.dynamic_index_in_dim(stacked, slot, 0, keepdims=False))
            return jnp.concatenate(taken, axis=1)

        cols = [columns_of(position // pair)]
        for n, perm in enumerate(perms):
            piece = columns_of((position ^ ((n + 1) * pair)) // pair)
            cols.append(lax.ppermute(piece, "ctx", perm))

        wide_out = array((length, width), f32)
        narrow_out = array((length, width), bf16)
        grad_q, part_k, part_v = call(
            back_kernel, (narrow_out, wide_out, wide_out), queries, key_rows, value_rows, d_attended, prefix
        )
        suffix = exclusive_sum(grad_block, position, n_ctx, False)
        grad_k, grad_v = call(suffix_kernel, (narrow_out, narrow_out), key_rows, value_rows, part_k, part_v, suffix)

        def weight_grad(core, dtype, *extra):
            row_tiles = 2 if width % (2 * HEAD_DIM) == 0 else 1
            out = pl.BlockSpec((width // row_tiles, own_cols), lambda i, at: (i, 0))
            return kernel_call(
                functools.partial(weight_grad_kernel, len(rows), len(extra)),
                core.reshape(1).astype(jnp.int32),
                *rows,
                *cols,
                *extra,
                out_shape=array((width, own_cols), dtype),
                grid_spec=pltpu.PrefetchScalarGridSpec(
                    num_scalar_prefetch=1,
                    grid=(row_tiles,),
                    in_specs=[pl.BlockSpec((length, width // row_tiles), lambda i, at: (0, i))] * len(rows)
                    + [pl.BlockSpec((length, own_cols), lambda i, at: (0, at[0]))] * len(cols)
                    + [out] * len(extra),
                    out_specs=out,
                ),
            )

        core = lax.rem(position, pair)
        if pair > 1:
            sent = weight_grad(1 - core, bf16)
            other = lax.ppermute(sent, "ctx", flipped(n_ctx, 1))
            grad_out_weight = weight_grad(core, f32, other)
        else:
            grad_out_weight = weight_grad(core, f32)
        return mixed, grad_q, grad_k, grad_v, grad_out_weight

    return body


def solution(mesh):
    n_ctx, n_head = mesh.shape["ctx"], mesh.shape["head"]
    body = make_body(n_ctx, n_head)

    return jax.shard_map(
        body,
        mesh=mesh,
        in_specs=(P("ctx", "head"),) * 3 + (P("head", None), P("ctx", "head")),
        out_specs=(P("ctx", "head"),) * 4 + (P("head", "ctx"),),
        check_vma=False,
    )
```

```python
import functools

import jax
import jax.numpy as jnp
from jax import lax
from jax.experimental import pallas as pl
from jax.experimental.pallas import tpu as pltpu
from jax.sharding import PartitionSpec as P


HEAD_DIM = 128

epsilon = 1e-06


bf16 = jnp.bfloat16
f32 = jnp.float32
VMEM = pl.BlockSpec(memory_space=pltpu.VMEM)
GRANT = 12 << 20


def mm(a, b, da, db):
    return lax.dot_general(a, b, (((da,), (db,)), ((), ())), preferred_element_type=f32)


def split(x):
    high = x.astype(bf16)
    return high, (x - high.astype(f32)).astype(bf16)


def head(h):
    return slice(h * HEAD_DIM, (h + 1) * HEAD_DIM)


def below(n):
    return lax.broadcasted_iota(jnp.int32, (n, n), 0) >= lax.broadcasted_iota(jnp.int32, (n, n), 1)


def array(shape, dtype):
    return jax.ShapeDtypeStruct(shape, dtype)


def kernel_call(kernel, *args, **settings):
    return pl.pallas_call(kernel, compiler_params=pltpu.CompilerParams(vmem_limit_bytes=GRANT), **settings)(*args)


def call(kernel, outs, *args):
    return kernel_call(
        kernel, *args, out_shape=outs, in_specs=[VMEM] * len(args), out_specs=jax.tree.map(lambda _: VMEM, outs)
    )


def state_kernel(k, v, out):
    for h in range(k.shape[1] // HEAD_DIM):
        out[head(h), :] = mm(k[:, head(h)], v[:, head(h)], 0, 0)


def intra_kernel(q, k, v, out):
    keep = below(q.shape[0])
    for h in range(q.shape[1] // HEAD_DIM):
        scores = jnp.where(keep, mm(q[:, head(h)], k[:, head(h)], 1, 1), 0.0).astype(bf16)
        out[:, head(h)] = mm(scores, v[:, head(h)], 1, 0)


def step_kernel(mask, upward, fresh, last, at, total, *refs):
    outer, other, outs = None if fresh else refs[0], refs[0 if fresh else 1], refs[1 if fresh else 2 :]
    value = other[...].astype(f32)
    outs[0][...] = jnp.zeros_like(value) if fresh else outer[...]
    upper = lax.rem(lax.div(at[1], mask), 2)

    @pl.when(upper == (1 if upward else 0))
    def _():
        outs[0][...] += value

    if not last:
        whole = total[...] + value
        outs[1][...] = whole
        outs[2][...] = whole.astype(bf16)


def row_scale_of(attended):
    return lax.rsqrt(jnp.mean(attended * attended, axis=-1, keepdims=True) + epsilon)


def norm_kernel(q, intra, prefix, attended, normed):
    for h in range(q.shape[1] // HEAD_DIM):
        high, low = split(prefix[head(h), :])
        query = q[:, head(h)]
        value = intra[:, head(h)] + mm(query, high, 1, 0) + mm(query, low, 1, 0)
        attended[:, head(h)] = value
        normed[:, head(h)] = (value * row_scale_of(value)).astype(bf16)


def block_at(ref, block, width):
    return ref[:, pl.ds(pl.multiple_of(block * width, width), width)]


def piece_kernel(block_of, at, weight, normed, *refs):
    extras, out = refs[:-1], refs[-1]
    value = mm(normed[...], block_at(weight, block_of(at[0]), out.shape[1]), 1, 0)
    for ref in extras:
        value = value + ref[...].astype(f32)
    out[...] = value.astype(bf16)


def add_terms(out, place, blocks, sources, weight):
    for ref, source in zip(blocks, sources):
        block, valid = source(place)

        @pl.when(valid)
        def _(ref=ref, block=block):
            out[...] += mm(ref[...], block_at(weight, block, ref.shape[1]), 1, 1)


def upstream_kernel(own, sources, at, weight, first, *refs):
    blocks, out = refs[:-1], refs[-1]
    if own:
        out[...] = mm(first[...], block_at(weight, at[0], first.shape[1]), 1, 1)
    else:
        out[...] = first[...]
    add_terms(out, at[0], blocks, sources, weight)


def finish_kernel(sources, at, weight, so_far, attended, q, *refs):
    blocks, (d_out, grad_out, upstream) = refs[:-3], refs[-3:]
    upstream[...] = so_far[...]
    add_terms(upstream, at[0], blocks, sources, weight)
    for h in range(d_out.shape[1] // HEAD_DIM):
        value, up = attended[:, head(h)], upstream[:, head(h)]
        scale = row_scale_of(value)
        unit = value * scale
        grad = scale * (up - unit * jnp.mean(up * unit, axis=-1, keepdims=True))
        grad = grad.astype(bf16)
        d_out[:, head(h)] = grad
        grad_out[head(h), :] = mm(q[:, head(h)], grad, 0, 0)


def pick_kernel(choices, at, *refs):
    sources, outs = refs[: len(refs) - len(choices)], refs[len(refs) - len(choices) :]
    for choice, out in zip(choices, outs):
        chosen = choice(at[0], at[1])
        for m, source in enumerate(sources):

            @pl.when(chosen == m)
            def _(out=out, source=source):
                out[...] = source[...]


def back_kernel(q, k, v, d, prefix, grad_q, part_k, part_v):
    keep = below(q.shape[0])
    for h in range(q.shape[1] // HEAD_DIM):
        qh, kh, vh, dh = q[:, head(h)], k[:, head(h)], v[:, head(h)], d[:, head(h)]
        high, low = split(prefix[head(h), :])
        scores = jnp.where(keep, mm(qh, kh, 1, 1), 0.0).astype(bf16)
        back = jnp.where(keep, mm(dh, vh, 1, 1), 0.0).astype(bf16)
        grad_q[:, head(h)] = (mm(back, kh, 1, 0) + mm(dh, high, 1, 1) + mm(dh, low, 1, 1)).astype(bf16)
        part_k[:, head(h)] = mm(back, qh, 0, 0)
        part_v[:, head(h)] = mm(scores, dh, 0, 0)


def suffix_kernel(k, v, part_k, part_v, suffix, grad_k, grad_v):
    for h in range(k.shape[1] // HEAD_DIM):
        high, low = split(suffix[head(h), :])
        kh, vh = k[:, head(h)], v[:, head(h)]
        grad_k[:, head(h)] = (part_k[:, head(h)] + mm(vh, high, 1, 1) + mm(vh, low, 1, 1)).astype(bf16)
        grad_v[:, head(h)] = (part_v[:, head(h)] + mm(kh, high, 1, 0) + mm(kh, low, 1, 0)).astype(bf16)


def weight_grad_kernel(count, core_of, at, *refs):
    rows, cols = refs[:count], refs[count : 2 * count]
    out = refs[-1]
    own_cols = out.shape[1]
    value = None
    for n in range(count):
        term = mm(rows[n][...], block_at(cols[n], core_of(at[1]), own_cols), 0, 0)
        value = term if value is None else value + term
    for ref in refs[2 * count : -1]:
        value = value + ref[...].astype(f32)
    out[...] = value.astype(out.dtype)


def flipped(size, mask):
    return [(i, i ^ mask) for i in range(size)]


def make_body(n_ctx, n_head):
    pair = min(2, n_ctx)
    chips = n_ctx // pair

    def body(queries, key_rows, value_rows, out_weight, cotangent):
        length, width = queries.shape
        model = out_weight.shape[1]
        part = model // n_head
        chip_cols = model // chips
        own_cols = chip_cols // pair
        position = lax.axis_index("ctx")
        place = lax.axis_index("head")
        wide = array((length, width), f32)
        narrow = array((length, width), bf16)
        piece = array((length, part), bf16)

        where = jnp.where(jnp.arange(2) == 0, place, position).astype(jnp.int32)

        def placed(kernel, outs, *args, scratch=()):
            return kernel_call(
                kernel,
                where,
                *args,
                out_shape=outs,
                in_specs=[pl.BlockSpec(memory_space=pltpu.SMEM)] + [VMEM] * len(args),
                out_specs=jax.tree.map(lambda _: VMEM, outs),
                scratch_shapes=scratch,
            )

        def exclusive_sum(block, upward):
            total, sent, outer, mask = block, block, [], 1
            state, state_sent = array(block.shape, f32), array(block.shape, bf16)
            while mask < n_ctx:
                other = lax.ppermute(sent, "ctx", flipped(n_ctx, mask))
                last = 2 * mask >= n_ctx
                got = placed(
                    functools.partial(step_kernel, mask, upward, not outer, last),
                    [state] if last else [state, state, state_sent],
                    total,
                    *outer,
                    other,
                )
                outer = [got[0]]
                if not last:
                    _, total, sent = got
                mask *= 2
            return outer[0] if outer else jnp.zeros_like(block)

        def line(r, p):
            over = []
            for link in range(p, n_head - 1, 2):
                if link - r + 1 >= 0:
                    over.append((link, link + 1))
                if link + r < n_head:
                    over.append((link + 1, link))
            return over

        def block_of(r, p, place):
            block = jnp.where(lax.rem(place, 2) == p, place + r, place - r)
            valid = (block >= 0) & (block < n_head)
            return jnp.minimum(jnp.maximum(block, 0), n_head - 1), valid

        rounds = [(r, p) for r in range(1, n_head) for p in range(2) if line(r, p)]
        got = {(0, 0): cotangent, (0, 1): cotangent}
        for r, p in rounds:
            if r < n_head - 1 or r == 1:
                got[r, p] = lax.ppermute(got[r - 1, 1 - p], "head", line(r, p))

        block_state = call(state_kernel, array((width, HEAD_DIM), f32), key_rows, value_rows)
        intra = call(intra_kernel, wide, queries, key_rows, value_rows)
        prefix = exclusive_sum(block_state, True)
        attended, normed = call(norm_kernel, (wide, narrow), queries, intra, prefix)

        def piece_of(block, *extras):
            kernel = functools.partial(piece_kernel, block)
            return placed(kernel, piece, out_weight, normed, *extras)

        came = {}
        for r, p in sorted(rounds, key=lambda at: -at[0]):
            extras = [came[r + 1, 1 - p]] if (r + 1, 1 - p) in came else []
            sent = piece_of(lambda i, r=r, p=p: block_of(r, p, i)[0], *extras)
            back = [(j, i) for i, j in line(r, p)]
            if (r, p) in got:
                came[r, p] = lax.ppermute(sent, "head", back)
            else:
                ends = [i for i, _ in back]

                def gives(place, position, ends=ends):
                    return functools.reduce(jnp.logical_or, [place == i for i in ends]).astype(jnp.int32)

                (sent,) = placed(functools.partial(pick_kernel, [gives]), [piece], got[r - 1, 1 - p], sent)
                got[r, p] = came[r, p] = lax.ppermute(sent, "head", line(r, p) + back)
        mixed = piece_of(lambda i: i, *[came[at] for at in ((1, 0), (1, 1)) if at in came])

        masks = list(range(pair, n_ctx, pair))
        rows_by = {0: normed}
        for mask in masks:
            low = mask & -mask
            high = mask ^ low
            if high == 0 or pair == 1:
                sent, via = normed, flipped(n_ctx, mask)
            else:
                (sent,) = placed(
                    functools.partial(pick_kernel, [lambda place, position: lax.rem(position, pair)]),
                    [narrow],
                    rows_by[high],
                    rows_by[low],
                )
                via = [(i, i ^ (low if i % pair == 0 else high)) for i in range(n_ctx)]
            rows_by[mask] = lax.ppermute(sent, "ctx", via)
        rows = [rows_by[mask] for mask in [0] + masks]

        def sources_of(here):
            return [functools.partial(block_of, *at) for at in here]

        upstream = cotangent
        for r in range(1, max(2, n_head - 1)):
            here = [at for at in rounds if at[0] == r and r < n_head - 1]
            upstream = placed(
                functools.partial(upstream_kernel, r == 1, sources_of(here)),
                wide,
                out_weight,
                upstream,
                *[got[at] for at in here],
            )
        here = [at for at in rounds if at[0] == n_head - 1]
        d_attended, grad_block = placed(
            functools.partial(finish_kernel, sources_of(here)),
            (narrow, array((width, HEAD_DIM), f32)),
            out_weight,
            upstream,
            attended,
            queries,
            *[got[at] for at in here],
            scratch=[pltpu.VMEM((length, width), f32)],
        )

        if chip_cols == part:

            def choice_of(mask, place, position):
                target = lax.div(position ^ mask, pair)
                chosen = jnp.int32(0)
                for n, at in enumerate(rounds):
                    block, valid = block_of(*at, place)
                    chosen = jnp.where(valid & (block == target), n + 1, chosen)
                return chosen

            cols = placed(
                functools.partial(pick_kernel, [functools.partial(choice_of, mask) for mask in [0] + masks]),
                [piece] * chips,
                cotangent,
                *[got[at] for at in rounds],
            )
        else:
            whole = jnp.zeros((n_head, length, part), bf16)
            whole = lax.dynamic_update_index_in_dim(whole, cotangent, place, 0)
            for at in rounds:
                block, valid = block_of(*at, place)
                old = lax.dynamic_index_in_dim(whole, block, 0, keepdims=False)
                whole = lax.dynamic_update_index_in_dim(whole, jnp.where(valid, got[at], old), block, 0)
            whole = whole.transpose(1, 0, 2).reshape(length, model)
            starts = [lax.div(position ^ mask, pair) * chip_cols for mask in [0] + masks]
            cols = [lax.dynamic_slice(whole, (0, start), (length, chip_cols)) for start in starts]
        cols = list(cols)
        for n, mask in enumerate(masks):
            cols[n + 1] = lax.ppermute(cols[n + 1], "ctx", flipped(n_ctx, mask))

        grad_q, part_k, part_v = call(
            back_kernel, (narrow, wide, wide), queries, key_rows, value_rows, d_attended, prefix
        )
        suffix = exclusive_sum(grad_block, False)
        grad_k, grad_v = call(suffix_kernel, (narrow, narrow), key_rows, value_rows, part_k, part_v, suffix)

        def weight_grad(core_of, dtype, span, *extra):
            return placed(
                functools.partial(weight_grad_kernel, len(rows[span]), core_of),
                array((width, own_cols), dtype),
                *rows[span],
                *cols[span],
                *extra,
            )

        def same(position):
            return lax.rem(position, pair)

        def partner(position):
            return 1 - lax.rem(position, pair)

        most, last = slice(0, max(1, chips - 1)), slice(max(1, chips - 1), chips)
        extra = []
        if pair > 1:
            if chips > 1:
                part_other = weight_grad(partner, f32, most)
                other = weight_grad(partner, bf16, last, part_other)
            else:
                other = weight_grad(partner, bf16, most)
            extra = [lax.ppermute(other, "ctx", flipped(n_ctx, 1))]
        if chips > 1:
            part_own = weight_grad(same, f32, most)
            grad_out_weight = weight_grad(same, f32, last, part_own, *extra)
        else:
            grad_out_weight = weight_grad(same, f32, most, *extra)
        return mixed, grad_q, grad_k, grad_v, grad_out_weight

    return body


def solution(mesh):
    n_ctx, n_head = mesh.shape["ctx"], mesh.shape["head"]
    body = make_body(n_ctx, n_head)

    return jax.shard_map(
        body,
        mesh=mesh,
        in_specs=(P("ctx", "head"),) * 3 + (P("head", None), P("ctx", "head")),
        out_specs=(P("ctx", "head"),) * 4 + (P("head", "ctx"),),
        check_vma=False,
    )
```

```python
import functools

import jax
import jax.numpy as jnp
from jax import lax
from jax.experimental import pallas as pl
from jax.experimental.pallas import tpu as pltpu
from jax.sharding import PartitionSpec as P


HEAD_DIM = 128

epsilon = 1e-06


bf16 = jnp.bfloat16
f32 = jnp.float32
VMEM = pl.BlockSpec(memory_space=pltpu.VMEM)
GRANT = 12 << 20


def mm(a, b, da, db):
    return lax.dot_general(a, b, (((da,), (db,)), ((), ())), preferred_element_type=f32)


def split(x):
    high = x.astype(bf16)
    return high, (x - high.astype(f32)).astype(bf16)


def head(h):
    return slice(h * HEAD_DIM, (h + 1) * HEAD_DIM)


def below(n):
    return lax.broadcasted_iota(jnp.int32, (n, n), 0) >= lax.broadcasted_iota(jnp.int32, (n, n), 1)


def array(shape, dtype):
    return jax.ShapeDtypeStruct(shape, dtype)


def kernel_call(kernel, *args, **settings):
    return pl.pallas_call(kernel, compiler_params=pltpu.CompilerParams(vmem_limit_bytes=GRANT), **settings)(*args)


def call(kernel, outs, *args):
    return kernel_call(
        kernel, *args, out_shape=outs, in_specs=[VMEM] * len(args), out_specs=jax.tree.map(lambda _: VMEM, outs)
    )


def state_kernel(k_far, v_far, out, k, v, sems):
    chunks = sems.shape[1]
    rows = k.shape[0] // chunks
    copies = []
    for n, (far, near) in enumerate(((k_far, k), (v_far, v))):
        for c in range(chunks):
            cut = pl.ds(c * rows, rows)
            copies.append(pltpu.make_async_copy(far.at[cut, :], near.at[cut, :], sems.at[n, c]))
            copies[-1].start()
    for copy in copies:
        copy.wait()
    for h in range(k.shape[1] // HEAD_DIM):
        out[head(h), :] = mm(k[:, head(h)], v[:, head(h)], 0, 0)


def intra_kernel(q, k, v, out):
    keep = below(q.shape[0])
    for h in range(q.shape[1] // HEAD_DIM):
        scores = jnp.where(keep, mm(q[:, head(h)], k[:, head(h)], 1, 1), 0.0).astype(bf16)
        out[:, head(h)] = mm(scores, v[:, head(h)], 1, 0)


def counts_at(at, mask, upward):
    return lax.rem(lax.div(at[1], mask), 2) == (1 if upward else 0)


def half_at(at, flip, rows):
    core = lax.rem(at[1], 2)
    return pl.ds(pl.multiple_of((1 - core if flip else core) * rows, rows), rows)


def core_step_kernel(upward, at, block, other, outer, *outs):
    outer[...] = jnp.zeros_like(outer)

    @pl.when(counts_at(at, 1, upward))
    def _():
        outer[...] = other[...]

    if outs:
        mine = half_at(at, False, outs[0].shape[0])
        total = block[mine, :] + other[mine, :]
        outs[0][...] = total.astype(bf16)
        for out in outs[1:]:
            out[...] = total


def chips_kernel(masks, upward, at, *refs):
    others, out = refs[:-1], refs[-1]
    out[...] = jnp.zeros_like(out)
    for mask, other in zip(masks, others):

        @pl.when(counts_at(at, 1 << (mask.bit_length() - 1), upward))
        def _(other=other):
            out[...] += other[...].astype(f32)


def step_kernel(mask, upward, fresh, last, at, total, *refs):
    outer, other, outs = None if fresh else refs[0], refs[0 if fresh else 1], refs[1 if fresh else 2 :]
    value = other[...].astype(f32)
    outs[0][...] = jnp.zeros_like(value) if fresh else outer[...]

    @pl.when(counts_at(at, mask, upward))
    def _():
        outs[0][...] += value

    if not last:
        whole = total[...] + value
        outs[1][...] = whole
        outs[2][...] = whole.astype(bf16)


def join_kernel(at, outer, mine, theirs, out):
    rows = mine.shape[0]
    here, there = half_at(at, False, rows), half_at(at, True, rows)
    out[here, :] = outer[here, :] + mine[...]
    out[there, :] = outer[there, :] + theirs[...]


def row_scale_of(attended):
    return lax.rsqrt(jnp.mean(attended * attended, axis=-1, keepdims=True) + epsilon)


def norm_kernel(q, intra, prefix, attended, normed):
    for h in range(q.shape[1] // HEAD_DIM):
        high, low = split(prefix[head(h), :])
        query = q[:, head(h)]
        value = intra[:, head(h)] + mm(query, high, 1, 0) + mm(query, low, 1, 0)
        attended[:, head(h)] = value
        normed[:, head(h)] = (value * row_scale_of(value)).astype(bf16)


def block_at(ref, block, width):
    return ref[:, pl.ds(pl.multiple_of(block * width, width), width)]


def piece_kernel(block_of, at, weight, normed, *refs):
    extras, out = refs[:-1], refs[-1]
    value = mm(normed[...], block_at(weight, block_of(at[0]), out.shape[1]), 1, 0)
    for ref in extras:
        value = value + ref[...].astype(f32)
    out[...] = value.astype(bf16)


def far_piece_kernel(block_of, at, weight, normed, out, buffer, sems):
    chunks, rows, part = buffer.shape
    columns = pl.ds(pl.multiple_of(block_of(at[0]) * part, part), part)
    copies = []
    for c in range(chunks):
        source = weight.at[pl.ds(c * rows, rows), columns]
        copies.append(pltpu.make_async_copy(source, buffer.at[c], sems.at[c]))
        copies[-1].start()
    value = None
    for c, copy in enumerate(copies):
        copy.wait()
        term = mm(normed[:, c * rows : (c + 1) * rows], buffer[c], 1, 0)
        value = term if value is None else value + term
    out[...] = value.astype(bf16)


def add_terms(out, place, blocks, sources, weight):
    for ref, source in zip(blocks, sources):
        block, valid = source(place)

        @pl.when(valid)
        def _(ref=ref, block=block):
            out[...] += mm(ref[...], block_at(weight, block, ref.shape[1]), 1, 1)


def upstream_kernel(own, sources, at, weight, first, *refs):
    blocks, out = refs[:-1], refs[-1]
    if own:
        out[...] = mm(first[...], block_at(weight, at[0], first.shape[1]), 1, 1)
    else:
        out[...] = first[...]
    add_terms(out, at[0], blocks, sources, weight)


def finish_kernel(sources, at, weight, so_far, attended, q, *refs):
    blocks, (d_out, grad_out, upstream) = refs[:-3], refs[-3:]
    upstream[...] = so_far[...]
    add_terms(upstream, at[0], blocks, sources, weight)
    for h in range(d_out.shape[1] // HEAD_DIM):
        value, up = attended[:, head(h)], upstream[:, head(h)]
        scale = row_scale_of(value)
        unit = value * scale
        grad = scale * (up - unit * jnp.mean(up * unit, axis=-1, keepdims=True))
        grad = grad.astype(bf16)
        d_out[:, head(h)] = grad
        grad_out[head(h), :] = mm(q[:, head(h)], grad, 0, 0)


def pick_kernel(choices, at, *refs):
    sources, outs = refs[: len(refs) - len(choices)], refs[len(refs) - len(choices) :]
    for choice, out in zip(choices, outs):
        chosen = choice(at[0], at[1])
        for m, source in enumerate(sources):

            @pl.when(chosen == m)
            def _(out=out, source=source):
                out[...] = source[...]


def back_kernel(q, k, v, d, prefix, grad_q, part_k, part_v):
    keep = below(q.shape[0])
    for h in range(q.shape[1] // HEAD_DIM):
        qh, kh, vh, dh = q[:, head(h)], k[:, head(h)], v[:, head(h)], d[:, head(h)]
        high, low = split(prefix[head(h), :])
        scores = jnp.where(keep, mm(qh, kh, 1, 1), 0.0).astype(bf16)
        back = jnp.where(keep, mm(dh, vh, 1, 1), 0.0).astype(bf16)
        grad_q[:, head(h)] = (mm(back, kh, 1, 0) + mm(dh, high, 1, 1) + mm(dh, low, 1, 1)).astype(bf16)
        part_k[:, head(h)] = mm(back, qh, 0, 0)
        part_v[:, head(h)] = mm(scores, dh, 0, 0)


def suffix_kernel(k, v, part_k, part_v, suffix, grad_k, grad_v):
    for h in range(k.shape[1] // HEAD_DIM):
        high, low = split(suffix[head(h), :])
        kh, vh = k[:, head(h)], v[:, head(h)]
        grad_k[:, head(h)] = (part_k[:, head(h)] + mm(vh, high, 1, 1) + mm(vh, low, 1, 1)).astype(bf16)
        grad_v[:, head(h)] = (part_v[:, head(h)] + mm(kh, high, 1, 0) + mm(kh, low, 1, 0)).astype(bf16)


def weight_all_kernel(*refs):
    count = len(refs) // 2
    rows, cols, out = refs[:count], refs[count:-1], refs[-1]
    value = mm(rows[0][...], cols[0][...], 0, 0)
    for n in range(1, count):
        value = value + mm(rows[n][...], cols[n][...], 0, 0)
    out[...] = value


def weight_last_kernel(core_of, at, so_far, rows, cols, *refs):
    extras, out = refs[:-1], refs[-1]
    core, own_cols = core_of(at[1]), out.shape[1]
    value = block_at(so_far, core, own_cols) + mm(rows[...], block_at(cols, core, own_cols), 0, 0)
    for ref in extras:
        value = value + ref[...].astype(f32)
    out[...] = value.astype(out.dtype)


def flipped(size, mask):
    return [(i, i ^ mask) for i in range(size)]


def make_body(n_ctx, n_head):
    pair = min(2, n_ctx)
    chips = n_ctx // pair

    def body(queries, key_rows, value_rows, out_weight, cotangent):
        length, width = queries.shape
        model = out_weight.shape[1]
        part = model // n_head
        chip_cols = model // chips
        own_cols = chip_cols // pair
        position = lax.axis_index("ctx")
        place = lax.axis_index("head")
        wide = array((length, width), f32)
        narrow = array((length, width), bf16)
        piece = array((length, part), bf16)

        where = jnp.where(jnp.arange(2) == 0, place, position).astype(jnp.int32)

        def placed(kernel, outs, *args, scratch=(), far=0):
            args = [pltpu.with_memory_space_constraint(x, pltpu.HBM) for x in args[:far]] + list(args[far:])
            specs = [pl.BlockSpec(memory_space=pltpu.HBM)] * far + [VMEM] * (len(args) - far)
            return kernel_call(
                kernel,
                where,
                *args,
                out_shape=outs,
                in_specs=[pl.BlockSpec(memory_space=pltpu.SMEM)] + specs,
                out_specs=jax.tree.map(lambda _: VMEM, outs),
                scratch_shapes=scratch,
            )

        def exclusive_sum(block, upward):
            if n_ctx == 1:
                return jnp.zeros_like(block)
            rows = block.shape[0] // 2
            state, state_sent = array((rows, HEAD_DIM), f32), array((rows, HEAD_DIM), bf16)
            other = lax.ppermute(block, "ctx", flipped(n_ctx, 1))
            direct = chips <= 4
            outs = [array(block.shape, f32)]
            if chips > 1:
                outs += [state_sent] if direct else [state_sent, state]
            on_chip = placed(functools.partial(core_step_kernel, upward), outs, block, other)
            if chips == 1:
                return on_chip[0]
            if direct:
                on_chip, sent = on_chip
                masks, others = range(2, n_ctx, 2), []
                for mask in masks:
                    others.append(lax.ppermute(sent, "ctx", flipped(n_ctx, mask)))
                (mine,) = placed(functools.partial(chips_kernel, masks, upward), [state], *others)
                theirs = lax.ppermute(mine, "ctx", flipped(n_ctx, 1))
                return placed(join_kernel, array(block.shape, f32), on_chip, mine, theirs)
            on_chip, sent, total = on_chip
            outer, mask = [], 2
            while mask < n_ctx:
                other = lax.ppermute(sent, "ctx", flipped(n_ctx, mask))
                last = 2 * mask >= n_ctx
                summed = placed(
                    functools.partial(step_kernel, mask, upward, not outer, last),
                    [state] if last else [state, state, state_sent],
                    total,
                    *outer,
                    other,
                )
                outer = [summed[0]]
                if not last:
                    _, total, sent = summed
                mask *= 2
            theirs = lax.ppermute(outer[0], "ctx", flipped(n_ctx, 1))
            return placed(join_kernel, array(block.shape, f32), on_chip, outer[0], theirs)

        def line(r, p):
            over = []
            for link in range(p, n_head - 1, 2):
                if link - r + 1 >= 0:
                    over.append((link, link + 1))
                if link + r < n_head:
                    over.append((link + 1, link))
            return over

        def block_of(r, p, place):
            block = jnp.where(lax.rem(place, 2) == p, place + r, place - r)
            valid = (block >= 0) & (block < n_head)
            return jnp.minimum(jnp.maximum(block, 0), n_head - 1), valid

        rounds = [(r, p) for r in range(1, n_head) for p in range(2) if line(r, p)]
        got = {(0, 0): cotangent, (0, 1): cotangent}
        for r, p in rounds:
            if r < n_head - 1 or r == 1:
                got[r, p] = lax.ppermute(got[r - 1, 1 - p], "head", line(r, p))

        far = pl.BlockSpec(memory_space=pltpu.HBM)
        block_state = kernel_call(
            state_kernel,
            pltpu.with_memory_space_constraint(key_rows, pltpu.HBM),
            pltpu.with_memory_space_constraint(value_rows, pltpu.HBM),
            out_shape=array((width, HEAD_DIM), f32),
            in_specs=[far, far],
            out_specs=VMEM,
            scratch_shapes=[
                pltpu.VMEM((length, width), bf16),
                pltpu.VMEM((length, width), bf16),
                pltpu.SemaphoreType.DMA((2, 4 if length % 64 == 0 else 1)),
            ],
        )
        intra = call(intra_kernel, wide, queries, key_rows, value_rows)
        prefix = exclusive_sum(block_state, True)
        attended, normed = call(norm_kernel, (wide, narrow), queries, intra, prefix)

        def piece_of(name, block, *extras):
            if not extras and name == f"piece_{n_head - 1}_0":
                chunks = 4 if width % (4 * HEAD_DIM) == 0 else 1
                scratch = [
                    pltpu.VMEM((chunks, width // chunks, part), bf16),
                    pltpu.SemaphoreType.DMA((chunks,)),
                ]
                kernel = functools.partial(far_piece_kernel, block)
                return placed(kernel, piece, out_weight, normed, scratch=scratch, far=1)
            kernel = functools.partial(piece_kernel, block)
            return placed(kernel, piece, out_weight, normed, *extras)

        came = {}
        for r, p in sorted(rounds, key=lambda at: -at[0]):
            extras = [came[r + 1, 1 - p]] if (r + 1, 1 - p) in came else []
            sent = piece_of(f"piece_{r}_{p}", lambda i, r=r, p=p: block_of(r, p, i)[0], *extras)
            back = [(j, i) for i, j in line(r, p)]
            if (r, p) in got:
                came[r, p] = lax.ppermute(sent, "head", back)
            else:
                ends = [i for i, _ in back]

                def gives(place, position, ends=ends):
                    return functools.reduce(jnp.logical_or, [place == i for i in ends]).astype(jnp.int32)

                (sent,) = placed(functools.partial(pick_kernel, [gives]), [piece], got[r - 1, 1 - p], sent)
                got[r, p] = came[r, p] = lax.ppermute(sent, "head", line(r, p) + back)
        mixed = piece_of("piece_last", lambda i: i, *[came[at] for at in ((1, 0), (1, 1)) if at in came])

        masks = list(range(pair, n_ctx, pair))
        rows_by = {0: normed}
        for mask in masks:
            low = mask & -mask
            high = mask ^ low
            if high == 0 or pair == 1:
                sent, via = normed, flipped(n_ctx, mask)
            else:
                (sent,) = placed(
                    functools.partial(pick_kernel, [lambda place, position: lax.rem(position, pair)]),
                    [narrow],
                    rows_by[high],
                    rows_by[low],
                )
                via = [(i, i ^ (low if i % pair == 0 else high)) for i in range(n_ctx)]
            rows_by[mask] = lax.ppermute(sent, "ctx", via)
        rows = [rows_by[mask] for mask in [0] + masks]

        def sources_of(here):
            return [functools.partial(block_of, *at) for at in here]

        upstream = placed(functools.partial(upstream_kernel, True, []), wide, out_weight, cotangent)
        for r in range(1, n_head - 1):
            here = [at for at in rounds if at[0] == r]
            upstream = placed(
                functools.partial(upstream_kernel, False, sources_of(here)),
                wide,
                out_weight,
                upstream,
                *[got[at] for at in here],
            )
        here = [at for at in rounds if at[0] == n_head - 1]
        d_attended, grad_block = placed(
            functools.partial(finish_kernel, sources_of(here)),
            (narrow, array((width, HEAD_DIM), f32)),
            out_weight,
            upstream,
            attended,
            queries,
            *[got[at] for at in here],
            scratch=[pltpu.VMEM((length, width), f32)],
        )

        if chip_cols == part:

            def choice_of(mask, place, position):
                target = lax.div(position ^ mask, pair)
                chosen = jnp.int32(0)
                for n, at in enumerate(rounds):
                    block, valid = block_of(*at, place)
                    chosen = jnp.where(valid & (block == target), n + 1, chosen)
                return chosen

            cols = placed(
                functools.partial(pick_kernel, [functools.partial(choice_of, mask) for mask in [0] + masks]),
                [piece] * chips,
                cotangent,
                *[got[at] for at in rounds],
            )
        else:
            whole = jnp.zeros((n_head, length, part), bf16)
            whole = lax.dynamic_update_index_in_dim(whole, cotangent, place, 0)
            for at in rounds:
                block, valid = block_of(*at, place)
                old = lax.dynamic_index_in_dim(whole, block, 0, keepdims=False)
                whole = lax.dynamic_update_index_in_dim(whole, jnp.where(valid, got[at], old), block, 0)
            whole = whole.transpose(1, 0, 2).reshape(length, model)
            starts = [lax.div(position ^ mask, pair) * chip_cols for mask in [0] + masks]
            cols = [lax.dynamic_slice(whole, (0, start), (length, chip_cols)) for start in starts]
        cols = list(cols)
        for n, mask in enumerate(masks):
            cols[n + 1] = lax.ppermute(cols[n + 1], "ctx", flipped(n_ctx, mask))

        grad_q, part_k, part_v = call(
            back_kernel, (narrow, wide, wide), queries, key_rows, value_rows, d_attended, prefix
        )
        suffix = exclusive_sum(grad_block, False)
        grad_k, grad_v = call(suffix_kernel, (narrow, narrow), key_rows, value_rows, part_k, part_v, suffix)

        def same(position):
            return lax.rem(position, pair)

        def partner(position):
            return 1 - lax.rem(position, pair)

        if chips > 1:
            whole = array((width, chip_cols), f32)
            so_far = call(weight_all_kernel, whole, *rows[:-1], *cols[:-1])
        else:
            so_far = jnp.zeros((width, chip_cols), f32)

        def weight_last(core_of, dtype, *extra):
            kernel = functools.partial(weight_last_kernel, core_of)
            return placed(kernel, array((width, own_cols), dtype), so_far, rows[-1], cols[-1], *extra)

        extra = []
        if pair > 1:
            other = weight_last(partner, bf16)
            extra = [lax.ppermute(other, "ctx", flipped(n_ctx, 1))]
        grad_out_weight = weight_last(same, f32, *extra)
        return mixed, grad_q, grad_k, grad_v, grad_out_weight

    return body


def solution(mesh):
    n_ctx, n_head = mesh.shape["ctx"], mesh.shape["head"]
    body = make_body(n_ctx, n_head)

    return jax.shard_map(
        body,
        mesh=mesh,
        in_specs=(P("ctx", "head"),) * 3 + (P("head", None), P("ctx", "head")),
        out_specs=(P("ctx", "head"),) * 4 + (P("head", "ctx"),),
        check_vma=False,
    )
```

```python
import functools

import jax
import jax.numpy as jnp
from jax import lax
from jax.experimental import pallas as pl
from jax.experimental.pallas import tpu as pltpu
from jax.sharding import PartitionSpec as P


HEAD_DIM = 128

epsilon = 1e-06


bf16 = jnp.bfloat16
f32 = jnp.float32
VMEM = pl.BlockSpec(memory_space=pltpu.VMEM)
GRANT = 12 << 20


def mm(a, b, da, db):
    return lax.dot_general(a, b, (((da,), (db,)), ((), ())), preferred_element_type=f32)


def split(x):
    high = x.astype(bf16)
    return high, (x - high.astype(f32)).astype(bf16)


def head(h):
    return slice(h * HEAD_DIM, (h + 1) * HEAD_DIM)


def below(n):
    return lax.broadcasted_iota(jnp.int32, (n, n), 0) >= lax.broadcasted_iota(jnp.int32, (n, n), 1)


def array(shape, dtype):
    return jax.ShapeDtypeStruct(shape, dtype)


def kernel_call(kernel, *args, **settings):
    return pl.pallas_call(kernel, compiler_params=pltpu.CompilerParams(vmem_limit_bytes=GRANT), **settings)(*args)


def call(kernel, outs, *args):
    return kernel_call(
        kernel, *args, out_shape=outs, in_specs=[VMEM] * len(args), out_specs=jax.tree.map(lambda _: VMEM, outs)
    )


def state_kernel(k_far, v_far, out, k, v, sems):
    chunks = sems.shape[1]
    rows = k.shape[0] // chunks
    copies = []
    for n, (far, near) in enumerate(((k_far, k), (v_far, v))):
        for c in range(chunks):
            cut = pl.ds(c * rows, rows)
            copies.append(pltpu.make_async_copy(far.at[cut, :], near.at[cut, :], sems.at[n, c]))
            copies[-1].start()
    for copy in copies:
        copy.wait()
    for h in range(k.shape[1] // HEAD_DIM):
        out[head(h), :] = mm(k[:, head(h)], v[:, head(h)], 0, 0)


def intra_kernel(q, k, v, out):
    keep = below(q.shape[0])
    for h in range(q.shape[1] // HEAD_DIM):
        scores = jnp.where(keep, mm(q[:, head(h)], k[:, head(h)], 1, 1), 0.0).astype(bf16)
        out[:, head(h)] = mm(scores, v[:, head(h)], 1, 0)


def counts_at(at, mask, upward):
    return lax.rem(lax.div(at[1], mask), 2) == (1 if upward else 0)


def half_at(at, flip, rows):
    core = lax.rem(at[1], 2)
    return pl.ds(pl.multiple_of((1 - core if flip else core) * rows, rows), rows)


def core_step_kernel(upward, at, block, other, outer, *outs):
    outer[...] = jnp.zeros_like(outer)

    @pl.when(counts_at(at, 1, upward))
    def _():
        outer[...] = other[...]

    if outs:
        mine = half_at(at, False, outs[0].shape[0])
        total = block[mine, :] + other[mine, :]
        outs[0][...] = total.astype(bf16)
        for out in outs[1:]:
            out[...] = total


def chips_kernel(masks, upward, at, *refs):
    others, out = refs[:-1], refs[-1]
    out[...] = jnp.zeros_like(out)
    for mask, other in zip(masks, others):

        @pl.when(counts_at(at, 1 << (mask.bit_length() - 1), upward))
        def _(other=other):
            out[...] += other[...].astype(f32)


def step_kernel(mask, upward, fresh, last, at, total, *refs):
    outer, other, outs = None if fresh else refs[0], refs[0 if fresh else 1], refs[1 if fresh else 2 :]
    value = other[...].astype(f32)
    outs[0][...] = jnp.zeros_like(value) if fresh else outer[...]

    @pl.when(counts_at(at, mask, upward))
    def _():
        outs[0][...] += value

    if not last:
        whole = total[...] + value
        outs[1][...] = whole
        outs[2][...] = whole.astype(bf16)


def join_kernel(at, outer, mine, theirs, out):
    rows = mine.shape[0]
    here, there = half_at(at, False, rows), half_at(at, True, rows)
    out[here, :] = outer[here, :] + mine[...]
    out[there, :] = outer[there, :] + theirs[...]


def row_scale_of(attended):
    return lax.rsqrt(jnp.mean(attended * attended, axis=-1, keepdims=True) + epsilon)


def norm_kernel(q, intra, prefix, attended, normed):
    for h in range(q.shape[1] // HEAD_DIM):
        high, low = split(prefix[head(h), :])
        query = q[:, head(h)]
        value = intra[:, head(h)] + mm(query, high, 1, 0) + mm(query, low, 1, 0)
        attended[:, head(h)] = value
        normed[:, head(h)] = (value * row_scale_of(value)).astype(bf16)


def block_at(ref, block, width):
    return ref[:, pl.ds(pl.multiple_of(block * width, width), width)]


def piece_kernel(block_of, at, weight, normed, *refs):
    extras, out = refs[:-1], refs[-1]
    value = mm(normed[...], block_at(weight, block_of(at[0]), out.shape[1]), 1, 0)
    for ref in extras:
        value = value + ref[...].astype(f32)
    out[...] = value.astype(bf16)


def far_piece_kernel(block_of, at, weight, normed, out, buffer, sems):
    chunks, rows, part = buffer.shape
    columns = pl.ds(pl.multiple_of(block_of(at[0]) * part, part), part)
    copies = []
    for c in range(chunks):
        source = weight.at[pl.ds(c * rows, rows), columns]
        copies.append(pltpu.make_async_copy(source, buffer.at[c], sems.at[c]))
        copies[-1].start()
    value = None
    for c, copy in enumerate(copies):
        copy.wait()
        term = mm(normed[:, c * rows : (c + 1) * rows], buffer[c], 1, 0)
        value = term if value is None else value + term
    out[...] = value.astype(bf16)


def add_terms(out, place, blocks, sources, weight):
    for ref, source in zip(blocks, sources):
        block, valid = source(place)

        @pl.when(valid)
        def _(ref=ref, block=block):
            out[...] += mm(ref[...], block_at(weight, block, ref.shape[1]), 1, 1)


def upstream_kernel(own, sources, at, weight, first, *refs):
    blocks, out = refs[:-1], refs[-1]
    if own:
        out[...] = mm(first[...], block_at(weight, at[0], first.shape[1]), 1, 1)
    else:
        out[...] = first[...]
    add_terms(out, at[0], blocks, sources, weight)


def finish_kernel(sources, at, weight, so_far, attended, q, *refs):
    blocks, (d_out, grad_out, upstream) = refs[:-3], refs[-3:]
    upstream[...] = so_far[...]
    add_terms(upstream, at[0], blocks, sources, weight)
    for h in range(d_out.shape[1] // HEAD_DIM):
        value, up = attended[:, head(h)], upstream[:, head(h)]
        scale = row_scale_of(value)
        unit = value * scale
        grad = scale * (up - unit * jnp.mean(up * unit, axis=-1, keepdims=True))
        grad = grad.astype(bf16)
        d_out[:, head(h)] = grad
        grad_out[head(h), :] = mm(q[:, head(h)], grad, 0, 0)


def pick_kernel(choices, at, *refs):
    sources, outs = refs[: len(refs) - len(choices)], refs[len(refs) - len(choices) :]
    for choice, out in zip(choices, outs):
        chosen = choice(at[0], at[1])
        for m, source in enumerate(sources):

            @pl.when(chosen == m)
            def _(out=out, source=source):
                out[...] = source[...]


def back_kernel(q, k, v, d, prefix, grad_q, part_k, part_v):
    keep = below(q.shape[0])
    for h in range(q.shape[1] // HEAD_DIM):
        qh, kh, vh, dh = q[:, head(h)], k[:, head(h)], v[:, head(h)], d[:, head(h)]
        high, low = split(prefix[head(h), :])
        scores = jnp.where(keep, mm(qh, kh, 1, 1), 0.0).astype(bf16)
        back = jnp.where(keep, mm(dh, vh, 1, 1), 0.0).astype(bf16)
        grad_q[:, head(h)] = (mm(back, kh, 1, 0) + mm(dh, high, 1, 1) + mm(dh, low, 1, 1)).astype(bf16)
        part_k[:, head(h)] = mm(back, qh, 0, 0)
        part_v[:, head(h)] = mm(scores, dh, 0, 0)


def suffix_kernel(k, v, part_k, part_v, suffix, grad_k, grad_v):
    for h in range(k.shape[1] // HEAD_DIM):
        high, low = split(suffix[head(h), :])
        kh, vh = k[:, head(h)], v[:, head(h)]
        grad_k[:, head(h)] = (part_k[:, head(h)] + mm(vh, high, 1, 1) + mm(vh, low, 1, 1)).astype(bf16)
        grad_v[:, head(h)] = (part_v[:, head(h)] + mm(kh, high, 1, 0) + mm(kh, low, 1, 0)).astype(bf16)


def weight_all_kernel(*refs):
    count = len(refs) // 2
    rows, cols, out = refs[:count], refs[count:-1], refs[-1]
    value = mm(rows[0][...], cols[0][...], 0, 0)
    for n in range(1, count):
        value = value + mm(rows[n][...], cols[n][...], 0, 0)
    out[...] = value


def weight_last_kernel(core_of, at, so_far, rows, cols, *refs):
    extras, out = refs[:-1], refs[-1]
    core, own_cols = core_of(at[1]), out.shape[1]
    value = block_at(so_far, core, own_cols) + mm(rows[...], block_at(cols, core, own_cols), 0, 0)
    for ref in extras:
        value = value + ref[...].astype(f32)
    out[...] = value.astype(out.dtype)


def weight_out_kernel(core_of, at, so_far, rows, cols, *refs):
    extras, (out, buffer, sems) = refs[:-3], refs[-3:]
    chunks, size, own_cols = buffer.shape
    core = core_of(at[1])
    mine = pl.ds(pl.multiple_of(core * own_cols, own_cols), own_cols)
    copies = []
    for c in range(chunks):
        cut = slice(c * size, (c + 1) * size)
        value = so_far[cut, mine] + mm(rows[:, cut], cols[:, mine], 0, 0)
        for ref in extras:
            value = value + ref[cut, :].astype(f32)
        buffer[c] = value
        copies.append(pltpu.make_async_copy(buffer.at[c], out.at[pl.ds(c * size, size), :], sems.at[c]))
        copies[-1].start()
    for copy in copies:
        copy.wait()


def flipped(size, mask):
    return [(i, i ^ mask) for i in range(size)]


def make_body(n_ctx, n_head):
    pair = min(2, n_ctx)
    chips = n_ctx // pair

    def body(queries, key_rows, value_rows, out_weight, cotangent):
        length, width = queries.shape
        model = out_weight.shape[1]
        part = model // n_head
        chip_cols = model // chips
        own_cols = chip_cols // pair
        position = lax.axis_index("ctx")
        place = lax.axis_index("head")
        wide = array((length, width), f32)
        narrow = array((length, width), bf16)
        piece = array((length, part), bf16)

        where = jnp.where(jnp.arange(2) == 0, place, position).astype(jnp.int32)

        def placed(kernel, outs, *args, scratch=(), far=0):
            args = [pltpu.with_memory_space_constraint(x, pltpu.HBM) for x in args[:far]] + list(args[far:])
            specs = [pl.BlockSpec(memory_space=pltpu.HBM)] * far + [VMEM] * (len(args) - far)
            return kernel_call(
                kernel,
                where,
                *args,
                out_shape=outs,
                in_specs=[pl.BlockSpec(memory_space=pltpu.SMEM)] + specs,
                out_specs=jax.tree.map(lambda _: VMEM, outs),
                scratch_shapes=scratch,
            )

        def exclusive_sum(block, upward):
            if n_ctx == 1:
                return jnp.zeros_like(block)
            rows = block.shape[0] // 2
            state, state_sent = array((rows, HEAD_DIM), f32), array((rows, HEAD_DIM), bf16)
            other = lax.ppermute(block, "ctx", flipped(n_ctx, 1))
            direct = chips <= 4
            outs = [array(block.shape, f32)]
            if chips > 1:
                outs += [state_sent] if direct else [state_sent, state]
            on_chip = placed(functools.partial(core_step_kernel, upward), outs, block, other)
            if chips == 1:
                return on_chip[0]
            if direct:
                on_chip, sent = on_chip
                masks, others = range(2, n_ctx, 2), []
                for mask in masks:
                    others.append(lax.ppermute(sent, "ctx", flipped(n_ctx, mask)))
                (mine,) = placed(functools.partial(chips_kernel, masks, upward), [state], *others)
                theirs = lax.ppermute(mine, "ctx", flipped(n_ctx, 1))
                return placed(join_kernel, array(block.shape, f32), on_chip, mine, theirs)
            on_chip, sent, total = on_chip
            outer, mask = [], 2
            while mask < n_ctx:
                other = lax.ppermute(sent, "ctx", flipped(n_ctx, mask))
                last = 2 * mask >= n_ctx
                summed = placed(
                    functools.partial(step_kernel, mask, upward, not outer, last),
                    [state] if last else [state, state, state_sent],
                    total,
                    *outer,
                    other,
                )
                outer = [summed[0]]
                if not last:
                    _, total, sent = summed
                mask *= 2
            theirs = lax.ppermute(outer[0], "ctx", flipped(n_ctx, 1))
            return placed(join_kernel, array(block.shape, f32), on_chip, outer[0], theirs)

        def line(r, p):
            over = []
            for link in range(p, n_head - 1, 2):
                if link - r + 1 >= 0:
                    over.append((link, link + 1))
                if link + r < n_head:
                    over.append((link + 1, link))
            return over

        def block_of(r, p, place):
            block = jnp.where(lax.rem(place, 2) == p, place + r, place - r)
            valid = (block >= 0) & (block < n_head)
            return jnp.minimum(jnp.maximum(block, 0), n_head - 1), valid

        rounds = [(r, p) for r in range(1, n_head) for p in range(2) if line(r, p)]
        got = {(0, 0): cotangent, (0, 1): cotangent}
        for r, p in rounds:
            if r < n_head - 1 or r == 1:
                got[r, p] = lax.ppermute(got[r - 1, 1 - p], "head", line(r, p))

        far = pl.BlockSpec(memory_space=pltpu.HBM)
        block_state = kernel_call(
            state_kernel,
            pltpu.with_memory_space_constraint(key_rows, pltpu.HBM),
            pltpu.with_memory_space_constraint(value_rows, pltpu.HBM),
            out_shape=array((width, HEAD_DIM), f32),
            in_specs=[far, far],
            out_specs=VMEM,
            scratch_shapes=[
                pltpu.VMEM((length, width), bf16),
                pltpu.VMEM((length, width), bf16),
                pltpu.SemaphoreType.DMA((2, 4 if length % 64 == 0 else 1)),
            ],
        )
        intra = call(intra_kernel, wide, queries, key_rows, value_rows)
        prefix = exclusive_sum(block_state, True)
        attended, normed = call(norm_kernel, (wide, narrow), queries, intra, prefix)

        def piece_of(name, block, *extras):
            if not extras and name == f"piece_{n_head - 1}_0":
                chunks = 4 if width % (4 * HEAD_DIM) == 0 else 1
                scratch = [
                    pltpu.VMEM((chunks, width // chunks, part), bf16),
                    pltpu.SemaphoreType.DMA((chunks,)),
                ]
                kernel = functools.partial(far_piece_kernel, block)
                return placed(kernel, piece, out_weight, normed, scratch=scratch, far=1)
            kernel = functools.partial(piece_kernel, block)
            return placed(kernel, piece, out_weight, normed, *extras)

        came = {}
        for r, p in sorted(rounds, key=lambda at: -at[0]):
            extras = [came[r + 1, 1 - p]] if (r + 1, 1 - p) in came else []
            sent = piece_of(f"piece_{r}_{p}", lambda i, r=r, p=p: block_of(r, p, i)[0], *extras)
            back = [(j, i) for i, j in line(r, p)]
            if (r, p) in got:
                came[r, p] = lax.ppermute(sent, "head", back)
            else:
                ends = [i for i, _ in back]

                def gives(place, position, ends=ends):
                    return functools.reduce(jnp.logical_or, [place == i for i in ends]).astype(jnp.int32)

                (sent,) = placed(functools.partial(pick_kernel, [gives]), [piece], got[r - 1, 1 - p], sent)
                got[r, p] = came[r, p] = lax.ppermute(sent, "head", line(r, p) + back)
        mixed = piece_of("piece_last", lambda i: i, *[came[at] for at in ((1, 0), (1, 1)) if at in came])

        masks = list(range(pair, n_ctx, pair))
        rows_by = {0: normed}
        for mask in masks:
            low = mask & -mask
            high = mask ^ low
            if high == 0 or pair == 1:
                sent, via = normed, flipped(n_ctx, mask)
            else:
                (sent,) = placed(
                    functools.partial(pick_kernel, [lambda place, position: lax.rem(position, pair)]),
                    [narrow],
                    rows_by[high],
                    rows_by[low],
                )
                via = [(i, i ^ (low if i % pair == 0 else high)) for i in range(n_ctx)]
            rows_by[mask] = lax.ppermute(sent, "ctx", via)
        rows = [rows_by[mask] for mask in [0] + masks]

        def sources_of(here):
            return [functools.partial(block_of, *at) for at in here]

        upstream = placed(functools.partial(upstream_kernel, True, []), wide, out_weight, cotangent)
        for r in range(1, n_head - 1):
            here = [at for at in rounds if at[0] == r]
            upstream = placed(
                functools.partial(upstream_kernel, False, sources_of(here)),
                wide,
                out_weight,
                upstream,
                *[got[at] for at in here],
            )
        here = [at for at in rounds if at[0] == n_head - 1]
        d_attended, grad_block = placed(
            functools.partial(finish_kernel, sources_of(here)),
            (narrow, array((width, HEAD_DIM), f32)),
            out_weight,
            upstream,
            attended,
            queries,
            *[got[at] for at in here],
            scratch=[pltpu.VMEM((length, width), f32)],
        )

        if chip_cols == part:

            def choice_of(mask, place, position):
                target = lax.div(position ^ mask, pair)
                chosen = jnp.int32(0)
                for n, at in enumerate(rounds):
                    block, valid = block_of(*at, place)
                    chosen = jnp.where(valid & (block == target), n + 1, chosen)
                return chosen

            cols = placed(
                functools.partial(pick_kernel, [functools.partial(choice_of, mask) for mask in [0] + masks]),
                [piece] * chips,
                cotangent,
                *[got[at] for at in rounds],
            )
        else:
            whole = jnp.zeros((n_head, length, part), bf16)
            whole = lax.dynamic_update_index_in_dim(whole, cotangent, place, 0)
            for at in rounds:
                block, valid = block_of(*at, place)
                old = lax.dynamic_index_in_dim(whole, block, 0, keepdims=False)
                whole = lax.dynamic_update_index_in_dim(whole, jnp.where(valid, got[at], old), block, 0)
            whole = whole.transpose(1, 0, 2).reshape(length, model)
            starts = [lax.div(position ^ mask, pair) * chip_cols for mask in [0] + masks]
            cols = [lax.dynamic_slice(whole, (0, start), (length, chip_cols)) for start in starts]
        cols = list(cols)
        for n, mask in enumerate(masks):
            cols[n + 1] = lax.ppermute(cols[n + 1], "ctx", flipped(n_ctx, mask))

        grad_q, part_k, part_v = call(
            back_kernel, (narrow, wide, wide), queries, key_rows, value_rows, d_attended, prefix
        )
        suffix = exclusive_sum(grad_block, False)
        grad_k, grad_v = call(suffix_kernel, (narrow, narrow), key_rows, value_rows, part_k, part_v, suffix)

        def same(position):
            return lax.rem(position, pair)

        def partner(position):
            return 1 - lax.rem(position, pair)

        if chips > 1:
            whole = array((width, chip_cols), f32)
            so_far = call(weight_all_kernel, whole, *rows[:-1], *cols[:-1])
        else:
            so_far = jnp.zeros((width, chip_cols), f32)

        def weight_last(core_of, dtype, *extra):
            kernel = functools.partial(weight_last_kernel, core_of)
            return placed(kernel, array((width, own_cols), dtype), so_far, rows[-1], cols[-1], *extra)

        extra = []
        if pair > 1:
            other = weight_last(partner, bf16)
            extra = [lax.ppermute(other, "ctx", flipped(n_ctx, 1))]
        pieces_out = 4 if width % (4 * HEAD_DIM) == 0 else 1
        grad_out_weight = kernel_call(
            functools.partial(weight_out_kernel, same),
            where,
            so_far,
            rows[-1],
            cols[-1],
            *extra,
            out_shape=array((width, own_cols), f32),
            in_specs=[pl.BlockSpec(memory_space=pltpu.SMEM)] + [VMEM] * (3 + len(extra)),
            out_specs=pl.BlockSpec(memory_space=pltpu.HBM),
            scratch_shapes=[
                pltpu.VMEM((pieces_out, width // pieces_out, own_cols), f32),
                pltpu.SemaphoreType.DMA((pieces_out,)),
            ],
        )
        return mixed, grad_q, grad_k, grad_v, grad_out_weight

    return body


def solution(mesh):
    n_ctx, n_head = mesh.shape["ctx"], mesh.shape["head"]
    body = make_body(n_ctx, n_head)

    return jax.shard_map(
        body,
        mesh=mesh,
        in_specs=(P("ctx", "head"),) * 3 + (P("head", None), P("ctx", "head")),
        out_specs=(P("ctx", "head"),) * 4 + (P("head", "ctx"),),
        check_vma=False,
    )
```
